32 devices in a mesh: grp: 2 (over x), comp: 16 (over z, y, core).
Axes of the slice: x: 2, y: 2, z: 4, core: 2. Of those that a mesh axis runs over, the one named last changes fastest.
Arguments:
- spectrum: float32 [1152, 96, 128], P(None, ('grp', 'comp')), parts along dimension 1, may hold values from 0.04 to 14, as said below
- sea_mask: int32 [96, 128], P(('grp', 'comp')), parts along dimension 0, may hold values 0 or 1
- ice_mask: int32 [96, 128], P(('grp', 'comp')), parts along dimension 0, may hold values 0 or 1
- wind: float32 [96, 128], P(('grp', 'comp')), parts along dimension 0, may hold values from 0.2 to 1
- source_matrix: bfloat16 [1152, 1152], replicated, may hold values from -0.1875 to 0.1875
Outputs:
- evolved: float32 [1152, 96, 128], P(None, ('grp', 'comp')), parts along dimension 1
The draws below stay inside these ranges and needn't reach their ends.
There are 2 independent parts, one for each index of `grp`. The reference program is written for one: setup_inputs(seed, part) draws one part's arguments, and reference() takes and returns one part's arrays. A program takes and returns all parts, laid end to end along the dimension named above; an argument that names none is the same for every part. Nothing has to cross between parts.
Inputs may be any that keep to these rules, and one draw needn't show every extreme that they name: `spectrum`: positive spectral densities.
All inputs are finite; a program needn't handle non-finite values. No bound on the sum of `sea_mask` or of `ice_mask` on one device may be relied on, other than what follows from the above.
Results may differ from the reference program's by a relative error of at most 0.0014.
Values sent between devices are 32-bit elements; how exact they have to be, the bound alone decides.
A program may use at most 64 MiB of HBM per device.

```python
import math
import jax
import jax.numpy as jnp

NDIR = 36
NFREQ = 32
K = 1152
NX = 128
NY = 48
STEPS = 2
SUBSTEPS = 3
SRC_SUB = 3


def draw_spectrum(key, part):
    base_key = jax.random.fold_in(key, 11)
    first_key, second_key, third_key = jax.random.split(base_key, 3)
    baseline = jax.random.uniform(first_key, (K, NY, NX), jnp.float32, 0.5, 1.5)
    cell_scale = jnp.exp(jax.random.uniform(second_key, (1, NY, NX), jnp.float32, math.log(0.3), math.log(3.0)))
    comp_scale = jnp.exp(jax.random.uniform(third_key, (K, 1, 1), jnp.float32, math.log(0.3), math.log(3.0)))
    return baseline * cell_scale * comp_scale


def with_ends(result, stream_key, least, high):
    dims = result.shape
    spot = [jax.random.randint(jax.random.fold_in(stream_key, axis), (), 0, dims[axis]) for axis in range(len(dims))]
    result = result.at[tuple(spot)].set(least)
    longest = dims.index(max(dims))
    spot[longest] = (spot[longest] + 1) % dims[longest]
    return result.at[tuple(spot)].set(high)


def levels(rng, dims, shards, low, high):
    def one(dim, blocks):
        heights = jax.random.uniform(jax.random.fold_in(jax.random.fold_in(rng, 6), dim), (blocks,), jnp.float32, low / len(shards), high / len(shards))
        return jnp.repeat(jnp.exp(heights), dims[dim] // blocks).reshape((-1,) + (1,) * (len(dims) - dim - 1))

    loudness = one(*shards[0])
    for cut in shards[1:]:
        loudness = loudness * one(*cut)
    return loudness


def centred(key, extent, deviation, limit, kind=jnp.bfloat16):
    values = jax.random.normal(key, extent, jnp.float32) * deviation
    return jnp.minimum(jnp.maximum(values, -limit), limit).astype(kind)


def setup_inputs(seed: int = 0, part: int = 0) -> dict:
    arg_keys = jax.random.split(jax.random.key(seed), 6)
    part_splits = jax.random.split(jax.random.fold_in(arg_keys[5], part), 6)
    spectrum = draw_spectrum(jax.random.fold_in(jax.random.fold_in(arg_keys[5], part), 71), part)
    sea_mask = with_ends((jax.random.randint(part_splits[1], (NY, NX), 0, 8) < 7).astype(jnp.int32), jax.random.fold_in(part_splits[1], 1), 0, 1)
    ice_mask = with_ends((jax.random.randint(part_splits[2], (NY, NX), 0, 6) < 1).astype(jnp.int32), jax.random.fold_in(part_splits[2], 1), 0, 1)
    wind = jnp.clip(0.2 + 0.8 * jax.random.uniform(part_splits[3], (NY, NX), jnp.float32) ** levels(part_splits[3], (NY, NX), ((0, 16),), -0.2, 0.2), 0.2, 1.0)
    source_matrix = centred(arg_keys[4], (K, K), K ** -0.5, 0.1875)
    return dict(spectrum=spectrum, sea_mask=sea_mask, ice_mask=ice_mask, wind=wind, source_matrix=source_matrix)


source_rate = 0.5
damping = 0.5


def courant(comp_index):
    direction = (comp_index % NDIR).astype(jnp.float32)
    frequency = (comp_index // NDIR).astype(jnp.float32)
    angles = 2.0 * jnp.pi * (direction + 0.5) / NDIR
    speeds = 0.6 * (0.35 + 0.65 * (NFREQ - 1 - frequency) / (NFREQ - 1))
    return (speeds * jnp.cos(angles))[:, None, None], (speeds * jnp.sin(angles))[:, None, None]


def advance(spectra, courant_x, courant_y):
    western = jnp.roll(spectra, 1, axis=2)
    eastern = jnp.roll(spectra, -1, axis=2)
    zero_row = jnp.zeros_like(spectra[:, :1])
    southern = jnp.concatenate([zero_row, spectra[:, :-1]], axis=1)
    northern = jnp.concatenate([spectra[:, 1:], zero_row], axis=1)
    staying = 1.0 - jnp.abs(courant_x) - jnp.abs(courant_y)
    return (staying * spectra + jnp.maximum(courant_x, 0.0) * western + jnp.maximum(-courant_x, 0.0) * eastern
            + jnp.maximum(courant_y, 0.0) * southern + jnp.maximum(-courant_y, 0.0) * northern)


def sources(spectra, sea, wind, source_matrix):
    layout_shape = spectra.shape
    flattened = spectra.reshape(layout_shape[0], -1)
    sea_flat = sea.reshape(1, -1)
    wind_flat = wind.reshape(1, -1)
    for source_step in range(SRC_SUB):
        rounded = flattened.astype(jnp.bfloat16)
        growth = jnp.dot(source_matrix, rounded, preferred_element_type=jnp.float32)
        energy = jnp.mean(flattened * flattened, axis=0, keepdims=True)
        flattened = sea_flat * (flattened + source_rate * wind_flat * growth) / (1.0 + damping * energy)
    return flattened.reshape(layout_shape)


def reference(spectrum, sea_mask, ice_mask, wind, source_matrix):
    sea = sea_mask.astype(jnp.float32)
    thaw = (1.0 - 0.5 * ice_mask.astype(jnp.float32))[None]
    courant_x, courant_y = courant(jnp.arange(K, dtype=jnp.int32))
    spectra = spectrum
    for outer_step in range(STEPS):
        for inner_step in range(SUBSTEPS):
            spectra = sea[None] * advance(spectra, courant_x, courant_y)
        spectra = sources(spectra, sea, wind, source_matrix) * thaw
    return spectra
```

```python
import functools

import jax
import jax.numpy as jnp
import numpy as np
from jax import lax
from jax.experimental import pallas as pl
from jax.experimental.pallas import tpu as pltpu
from jax.sharding import PartitionSpec as P

NDIR = 36
NFREQ = 32
K = NDIR * NFREQ
STEPS = 2
SUBSTEPS = 3
SRC_SUB = 3
RATE = 0.5
DAMPING = 0.5

HALF = NDIR // 2
QUARTER = HALF // 2
SIDE = HALF * NFREQ
CHUNKS = 3
PER = HALF // CHUNKS
SPAN = PER * NFREQ
TILE = 288
UP_ROW = (1, 2, 0)
DOWN_ROW = (1, 0, 2)
MESH = pl.DeviceIdType.MESH


def tables(width):
    frequency = np.arange(NFREQ, dtype=np.float64)
    speeds = 0.6 * (0.35 + 0.65 * (NFREQ - 1 - frequency) / (NFREQ - 1))
    angles = 2.0 * np.pi * (np.arange(HALF) + 0.5) / NDIR
    trig = np.concatenate([np.abs(np.cos(angles)), np.abs(np.sin(angles))])
    spread = lambda v: np.broadcast_to(v.astype(np.float32)[:, None], (v.size, width)).copy()
    return spread(speeds), spread(trig)


def strided(d):
    return pl.ds(d, NFREQ, stride=NDIR)


def kernel(size, spec, sea_ref, ice_ref, wind_ref, mat_hbm, speed_ref, trig_ref, out,
           nat, work, south, north, send_up, send_down, sea_south, sea_north, mat, low_mid, low_out,
           total, load_sem, mat_sem, mask_send, mask_recv, up_send, up_recv, down_send, down_recv, out_sem):
    rows, width = spec.shape[0], spec.shape[2]
    me = lax.axis_index("comp")
    has_south, has_north = me > 0, me < size - 1

    loads = [pltpu.make_async_copy(spec.at[r], nat.at[r], load_sem.at[r]) for r in range(rows)]
    for r in UP_ROW:
        loads[r].start()

    barrier = pltpu.get_barrier_semaphore()

    @pl.when(has_south)
    def _():
        pl.semaphore_signal(barrier, inc=1, device_id={"comp": me - 1}, device_id_type=MESH)

    @pl.when(has_north)
    def _():
        pl.semaphore_signal(barrier, inc=1, device_id={"comp": me + 1}, device_id_type=MESH)

    def up_copy(step, p, h):
        part = pl.ds(h * SPAN, SPAN)
        return pltpu.make_async_remote_copy(
            src_ref=send_up.at[step, p, part], dst_ref=south.at[step, p, part],
            send_sem=up_send.at[step, p, h], recv_sem=up_recv.at[step, p, h],
            device_id={"comp": me + 1}, device_id_type=MESH)

    def down_copy(step, p, h):
        part = pl.ds(h * SPAN, SPAN)
        return pltpu.make_async_remote_copy(
            src_ref=send_down.at[step, p, part], dst_ref=north.at[step, p, part],
            send_sem=down_send.at[step, p, h], recv_sem=down_recv.at[step, p, h],
            device_id={"comp": me - 1}, device_id_type=MESH)

    def pack(step, p):
        for d in range(HALF):
            send_up[step, p, pl.ds(d * NFREQ, NFREQ), :] = nat[UP_ROW[p], strided(d), :]
            send_down[step, p, pl.ds(d * NFREQ, NFREQ), :] = nat[DOWN_ROW[p], strided(d + HALF), :]

    def send(step, p):
        @pl.when(has_north)
        def _():
            for h in range(CHUNKS):
                up_copy(step, p, h).start()

        @pl.when(has_south)
        def _():
            for h in range(CHUNKS):
                down_copy(step, p, h).start()

    def receive(step, p, h):
        @pl.when(has_south)
        def _():
            up_copy(step, p, h).wait_recv()

        @pl.when(has_north)
        def _():
            down_copy(step, p, h).wait_recv()

    def mask_up():
        return pltpu.make_async_remote_copy(
            src_ref=sea_ref, dst_ref=sea_south, send_sem=mask_send.at[0], recv_sem=mask_recv.at[0],
            device_id={"comp": me + 1}, device_id_type=MESH)

    def mask_down():
        return pltpu.make_async_remote_copy(
            src_ref=sea_ref, dst_ref=sea_north, send_sem=mask_send.at[1], recv_sem=mask_recv.at[1],
            device_id={"comp": me - 1}, device_id_type=MESH)

    loads[1].wait()
    pack(0, 0)
    pl.semaphore_wait(barrier, has_south.astype(jnp.int32) + has_north.astype(jnp.int32))

    @pl.when(has_north)
    def _():
        mask_up().start()

    @pl.when(has_south)
    def _():
        mask_down().start()

    send(0, 0)
    loads[2].wait()
    loads[0].wait()
    mat_load = pltpu.make_async_copy(mat_hbm, mat, mat_sem)
    mat_load.start()
    for p in range(1, rows):
        pack(0, p)
        send(0, p)

    @pl.when(jnp.logical_not(has_south))
    def _():
        sea_south[...] = jnp.zeros_like(sea_south)
        south[...] = jnp.zeros_like(south)

    @pl.when(jnp.logical_not(has_north))
    def _():
        sea_north[...] = jnp.zeros_like(sea_north)
        north[...] = jnp.zeros_like(north)

    @pl.when(has_south)
    def _():
        mask_up().wait_recv()

    @pl.when(has_north)
    def _():
        mask_down().wait_recv()

    sea = [sea_ref[pl.ds(r, 1), :].astype(jnp.float32) for r in range(rows)]
    below = [sea_south[pl.ds(rows - 2 + r, 1), :].astype(jnp.float32) for r in range(2)]
    above = [sea_north[pl.ds(1 - r, 1), :].astype(jnp.float32) for r in range(2)]
    thaw = [1.0 - 0.5 * ice_ref[pl.ds(r, 1), :].astype(jnp.float32) for r in range(rows)]
    gain = [RATE * wind_ref[pl.ds(r, 1), :] for r in range(rows)]
    far_up = sea[0] * below[0] * below[1]
    far_down = sea[rows - 1] * above[0] * above[1]

    def courant(d):
        speed = speed_ref[...]
        return speed * trig_ref[pl.ds(d, 1), :], speed * trig_ref[pl.ds(HALF + d, 1), :]

    def advance(step, d, up_shift, down_shift):
        cx, cy = courant(d)
        staying = 1.0 - cx - cy
        halo = pl.ds(pl.multiple_of(d * NFREQ, NFREQ), NFREQ)
        sides = ((south, below + sea, d, up_shift), (north, above + sea[::-1], d + HALF, down_shift))
        for edge, seas, first_row, shift in sides:
            order = list(range(rows)) if edge is south else list(range(rows))[::-1]
            lines = [edge[step, 0, halo, :], edge[step, 1, halo, :]]
            lines += [nat[r, strided(first_row), :] for r in order]
            for s in range(SUBSTEPS):
                moved = []
                for i in range(s, len(lines)):
                    value = staying * lines[i] + cx * pltpu.roll(lines[i], shift, 1)
                    if i > 0:
                        value = value + cy * lines[i - 1]
                    moved.append(seas[i] * value)
                lines = lines[:s] + moved
            for r, line in zip(order, lines[2:]):
                work[r, strided(first_row), :] = line

    def advance_chunk(step, h):
        for start in range(h * PER, (h + 1) * PER, CHUNKS):
            eastward = start < QUARTER
            shifts = (1, width - 1) if eastward else (width - 1, 1)

            def one(i, carry):
                advance(step, start + i, *shifts)
                return carry

            lax.fori_loop(0, CHUNKS, one, 0)

    def far_chunk(step, h):
        def one(i, carry):
            d = h * PER + i
            _, cy = courant(d)
            cube = cy * cy * cy
            halo = pl.ds(pl.multiple_of(d * NFREQ, NFREQ), NFREQ)
            work[0, strided(d), :] += (cube * far_up) * south[step, 2, halo, :]
            work[rows - 1, strided(d + HALF), :] += (cube * far_down) * north[step, 2, halo, :]
            return carry

        lax.fori_loop(0, PER, one, 0)

    def fold(value):
        return jnp.sum(value.reshape(-1, 8, width), axis=0)

    def prepare(which, low):
        for j, r in enumerate(which):
            total[r] = jnp.zeros((8, width), jnp.float32)
            for t in range(K // TILE):
                part = pl.ds(t * TILE, TILE)
                value = work[r, part, :]
                low[0, part, pl.ds(j * width, width)] = value.astype(jnp.bfloat16)
                total[r] += fold(value * value)

    def sources(which, low, finish=None):
        for sub in range(SRC_SUB):
            now, later = sub % 2, (sub + 1) % 2
            last = sub == SRC_SUB - 1
            scale = []
            for r in which:
                energy = jnp.sum(total[r], axis=0, keepdims=True) * (1.0 / K)
                factor = sea[r] / (1.0 + DAMPING * energy)
                scale.append(factor * thaw[r] if last else factor)
                total[r] = jnp.zeros((8, width), jnp.float32)
            for t in range(K // TILE):
                part = pl.ds(t * TILE, TILE)
                growth = jnp.dot(mat[part, :], low[now], preferred_element_type=jnp.float32)
                for j, r in enumerate(which):
                    value = (work[r, part, :] + gain[r] * growth[:, j * width:(j + 1) * width]) * scale[j]
                    if last:
                        nat[r, part, :] = value
                    else:
                        work[r, part, :] = value
                        low[later, part, pl.ds(j * width, width)] = value.astype(jnp.bfloat16)
                        total[r] += fold(value * value)
                if last and finish is not None:
                    finish(t)

    def out_copy(r, t):
        part = pl.ds(t * TILE, TILE)
        return pltpu.make_async_copy(nat.at[r, part], out.at[r, part], out_sem.at[r, t])

    for step in range(STEPS):
        last = step == STEPS - 1
        for h in range(CHUNKS):
            receive(step, 0, h)
            receive(step, 1, h)
            advance_chunk(step, h)
        if step == 0:
            mat_load.wait()
        prepare((1,), low_mid)
        sources((1,), low_mid, (lambda t: out_copy(1, t).start()) if last else None)
        if not last:
            pack(step + 1, 0)
            send(step + 1, 0)
        for h in range(CHUNKS):
            receive(step, 2, h)
            far_chunk(step, h)
        prepare((0, 2), low_out)

        def finish(t):
            out_copy(0, t).start()
            out_copy(2, t).start()

        sources((0, 2), low_out, finish if last else None)
        if not last:
            for p in range(1, rows):
                pack(step + 1, p)
                send(step + 1, p)

    @pl.when(has_north)
    def _():
        mask_up().wait_send()
        for step in range(STEPS):
            for p in range(rows):
                for h in range(CHUNKS):
                    up_copy(step, p, h).wait_send()

    @pl.when(has_south)
    def _():
        mask_down().wait_send()
        for step in range(STEPS):
            for p in range(rows):
                for h in range(CHUNKS):
                    down_copy(step, p, h).wait_send()

    for r in range(rows):
        for t in range(K // TILE):
            out_copy(r, t).wait()


def on_device(spectrum, sea_mask, ice_mask, wind, source_matrix):
    size = lax.axis_size("comp")
    spectra = spectrum.transpose(1, 0, 2)
    rows, _, width = spectra.shape
    speeds, trig = (jnp.asarray(t) for t in tables(width))
    hbm = pl.BlockSpec(memory_space=pl.ANY)
    vmem = pl.BlockSpec(memory_space=pltpu.VMEM)
    dma = pltpu.SemaphoreType.DMA
    full = pltpu.VMEM((rows, K, width), jnp.float32)
    halo = pltpu.VMEM((STEPS, rows, SIDE, width), jnp.float32)
    pieces = dma((STEPS, rows, CHUNKS))
    result = pl.pallas_call(
        functools.partial(kernel, size),
        out_shape=jax.ShapeDtypeStruct(spectra.shape, jnp.float32),
        in_specs=[hbm, vmem, vmem, vmem, hbm, vmem, vmem],
        out_specs=hbm,
        scratch_shapes=[
            full, full, halo, halo, halo, halo,
            pltpu.VMEM(sea_mask.shape, jnp.int32),
            pltpu.VMEM(sea_mask.shape, jnp.int32),
            pltpu.VMEM((K, K), jnp.bfloat16),
            pltpu.VMEM((2, K, width), jnp.bfloat16),
            pltpu.VMEM((2, K, 2 * width), jnp.bfloat16),
            pltpu.VMEM((rows, 8, width), jnp.float32),
            dma((rows,)), dma, dma((2,)), dma((2,)),
            pieces, pieces, pieces, pieces,
            dma((rows, K // TILE)),
        ],
        compiler_params=pltpu.CompilerParams(
            collective_id=0, has_side_effects=True, vmem_limit_bytes=56 * 1024 * 1024),
        name="wave",
    )(spectra, sea_mask, ice_mask, wind, source_matrix, speeds, trig)
    return result.transpose(1, 0, 2)


def solution(mesh):
    return jax.shard_map(
        on_device,
        mesh=mesh,
        in_specs=(
            P(None, ("grp", "comp"), None),
            P(("grp", "comp"), None),
            P(("grp", "comp"), None),
            P(("grp", "comp"), None),
            P(),
        ),
        out_specs=P(None, ("grp", "comp"), None),
        check_vma=False,
    )
```

```python
import functools

import jax
import jax.numpy as jnp
import numpy as np
from jax import lax
from jax.experimental import pallas as pl
from jax.experimental.pallas import tpu as pltpu
from jax.sharding import PartitionSpec as P

NDIR = 36
NFREQ = 32
K = NDIR * NFREQ
STEPS = 2
SUBSTEPS = 3
SRC_SUB = 3
RATE = 0.5
DAMPING = 0.5

HALF = NDIR // 2
QUARTER = HALF // 2
SIDE = HALF * NFREQ
CHUNKS = 3
PER = HALF // CHUNKS
SPAN = PER * NFREQ
TILE = 288
UP_ROW = (1, 2, 0)
DOWN_ROW = (1, 0, 2)
FOLD = 4
UNITS = 3 * CHUNKS
RELAYED = 9
MESH = pl.DeviceIdType.MESH


def tables(width):
    frequency = np.arange(NFREQ, dtype=np.float64)
    speeds = 0.6 * (0.35 + 0.65 * (NFREQ - 1 - frequency) / (NFREQ - 1))
    angles = 2.0 * np.pi * (np.arange(HALF) + 0.5) / NDIR
    trig = np.concatenate([np.abs(np.cos(angles)), np.abs(np.sin(angles))])
    spread = lambda v: np.broadcast_to(v.astype(np.float32)[:, None], (v.size, width)).copy()
    return spread(speeds), spread(trig)


def strided(d):
    return pl.ds(d, NFREQ, stride=NDIR)


def kernel(size, folded, spec, sea_ref, ice_ref, wind_ref, mat_hbm, speed_ref, trig_ref, out,
           nat, work, south, north, send_up, send_down, sea_south, sea_north, mat, low_mid, low_out,
           total, parcel, load_sem, mat_sem, mask_send, mask_recv, up_send, up_recv, down_send, down_recv, leg_recv, hop_send, out_sem):
    rows, width = spec.shape[0], spec.shape[2]
    me = lax.axis_index("comp")
    has_south, has_north = me > 0, me < size - 1
    pos, fold_at, folds = me % FOLD, me // FOLD, size // FOLD
    lower, upper = pos == 0, pos == FOLD - 1
    later_fold, prior_fold = fold_at < folds - 1, fold_at > 0
    share_up = (RELAYED * (folds - 1 - fold_at) + folds // 2) // folds
    share_down = (RELAYED * fold_at + folds // 2) // folds
    greeted = has_south.astype(jnp.int32) + has_north.astype(jnp.int32)

    loads = [pltpu.make_async_copy(spec.at[r], nat.at[r], load_sem.at[r]) for r in range(rows)]
    for r in UP_ROW:
        loads[r].start()

    barrier = pltpu.get_barrier_semaphore()

    @pl.when(has_south)
    def _():
        pl.semaphore_signal(barrier, inc=1, device_id={"comp": me - 1}, device_id_type=MESH)

    @pl.when(has_north)
    def _():
        pl.semaphore_signal(barrier, inc=1, device_id={"comp": me + 1}, device_id_type=MESH)

    if folded:
        hellos = ((lower, FOLD - 1), (upper, 1 - FOLD))
        hellos += tuple((jnp.logical_and(end, near), way) for end in (lower, upper)
                        for near, way in ((later_fold, FOLD), (prior_fold, -FOLD)))
        for there, way in hellos:
            @pl.when(there)
            def _():
                pl.semaphore_signal(barrier, inc=1, device_id={"comp": me + way}, device_id_type=MESH)

            greeted += there.astype(jnp.int32)

    def relayed(share, p, h):
        return ((p * CHUNKS + h) * share) % UNITS < share

    def leg(source, step, p, h, send_sem, way):
        part = pl.ds(h * SPAN, SPAN)
        return pltpu.make_async_remote_copy(
            src_ref=source.at[step, p, part], dst_ref=parcel.at[step, p, part],
            send_sem=send_sem.at[step, p, h], recv_sem=leg_recv.at[step, p, h],
            device_id={"comp": me + way}, device_id_type=MESH)

    def hop(target, step, p, h, recv_sem, way):
        part = pl.ds(h * SPAN, SPAN)
        return pltpu.make_async_remote_copy(
            src_ref=parcel.at[step, p, part], dst_ref=target.at[step, p, part],
            send_sem=hop_send.at[step, p, h], recv_sem=recv_sem.at[step, p, h],
            device_id={"comp": me + way}, device_id_type=MESH)

    def relay(step, p):
        if not folded:
            return
        for h in range(CHUNKS):
            @pl.when(lower & later_fold & relayed(share_up, p, h))
            def _():
                leg(send_up, step, p, h, up_send, 1 - FOLD).wait_recv()
                hop(south, step, p, h, up_recv, FOLD).start()

            @pl.when(upper & prior_fold & relayed(share_down, p, h))
            def _():
                leg(send_down, step, p, h, down_send, FOLD - 1).wait_recv()
                hop(north, step, p, h, down_recv, -FOLD).start()

    def relay_done(step, p):
        if not folded:
            return
        for h in range(CHUNKS):
            @pl.when(lower & later_fold & relayed(share_up, p, h))
            def _():
                hop(south, step, p, h, up_recv, FOLD).wait_send()

            @pl.when(upper & prior_fold & relayed(share_down, p, h))
            def _():
                hop(north, step, p, h, down_recv, -FOLD).wait_send()

    def up_copy(step, p, h):
        part = pl.ds(h * SPAN, SPAN)
        return pltpu.make_async_remote_copy(
            src_ref=send_up.at[step, p, part], dst_ref=south.at[step, p, part],
            send_sem=up_send.at[step, p, h], recv_sem=up_recv.at[step, p, h],
            device_id={"comp": me + 1}, device_id_type=MESH)

    def down_copy(step, p, h):
        part = pl.ds(h * SPAN, SPAN)
        return pltpu.make_async_remote_copy(
            src_ref=send_down.at[step, p, part], dst_ref=north.at[step, p, part],
            send_sem=down_send.at[step, p, h], recv_sem=down_recv.at[step, p, h],
            device_id={"comp": me - 1}, device_id_type=MESH)

    def pack(step, p):
        for d in range(HALF):
            send_up[step, p, pl.ds(d * NFREQ, NFREQ), :] = nat[UP_ROW[p], strided(d), :]
            send_down[step, p, pl.ds(d * NFREQ, NFREQ), :] = nat[DOWN_ROW[p], strided(d + HALF), :]

    def send(step, p):
        for h in range(CHUNKS):
            by_up, by_down = has_north, has_south
            if folded:
                aside = upper & has_north & relayed(share_up, p, h)
                by_up = has_north & jnp.logical_not(aside)

                @pl.when(aside)
                def _():
                    leg(send_up, step, p, h, up_send, 1 - FOLD).start()

                aside = lower & has_south & relayed(share_down, p, h)
                by_down = has_south & jnp.logical_not(aside)

                @pl.when(aside)
                def _():
                    leg(send_down, step, p, h, down_send, FOLD - 1).start()

            @pl.when(by_up)
            def _():
                up_copy(step, p, h).start()

            @pl.when(by_down)
            def _():
                down_copy(step, p, h).start()

    def receive(step, p, h):
        @pl.when(has_south)
        def _():
            up_copy(step, p, h).wait_recv()

        @pl.when(has_north)
        def _():
            down_copy(step, p, h).wait_recv()

    def mask_up():
        return pltpu.make_async_remote_copy(
            src_ref=sea_ref, dst_ref=sea_south, send_sem=mask_send.at[0], recv_sem=mask_recv.at[0],
            device_id={"comp": me + 1}, device_id_type=MESH)

    def mask_down():
        return pltpu.make_async_remote_copy(
            src_ref=sea_ref, dst_ref=sea_north, send_sem=mask_send.at[1], recv_sem=mask_recv.at[1],
            device_id={"comp": me - 1}, device_id_type=MESH)

    loads[1].wait()
    pack(0, 0)
    pl.semaphore_wait(barrier, greeted)

    @pl.when(has_north)
    def _():
        mask_up().start()

    @pl.when(has_south)
    def _():
        mask_down().start()

    send(0, 0)
    loads[2].wait()
    loads[0].wait()
    mat_load = pltpu.make_async_copy(mat_hbm, mat, mat_sem)
    mat_load.start()
    for p in range(1, rows):
        pack(0, p)
        send(0, p)

    @pl.when(jnp.logical_not(has_south))
    def _():
        sea_south[...] = jnp.zeros_like(sea_south)
        south[...] = jnp.zeros_like(south)

    @pl.when(jnp.logical_not(has_north))
    def _():
        sea_north[...] = jnp.zeros_like(sea_north)
        north[...] = jnp.zeros_like(north)

    @pl.when(has_south)
    def _():
        mask_up().wait_recv()

    @pl.when(has_north)
    def _():
        mask_down().wait_recv()

    sea = [sea_ref[pl.ds(r, 1), :].astype(jnp.float32) for r in range(rows)]
    below = [sea_south[pl.ds(rows - 2 + r, 1), :].astype(jnp.float32) for r in range(2)]
    above = [sea_north[pl.ds(1 - r, 1), :].astype(jnp.float32) for r in range(2)]
    thaw = [1.0 - 0.5 * ice_ref[pl.ds(r, 1), :].astype(jnp.float32) for r in range(rows)]
    gain = [RATE * wind_ref[pl.ds(r, 1), :] for r in range(rows)]
    far_up = sea[0] * below[0] * below[1]
    far_down = sea[rows - 1] * above[0] * above[1]

    def courant(d):
        speed = speed_ref[...]
        return speed * trig_ref[pl.ds(d, 1), :], speed * trig_ref[pl.ds(HALF + d, 1), :]

    def advance(step, d, up_shift, down_shift):
        cx, cy = courant(d)
        staying = 1.0 - cx - cy
        halo = pl.ds(pl.multiple_of(d * NFREQ, NFREQ), NFREQ)
        sides = ((south, below + sea, d, up_shift), (north, above + sea[::-1], d + HALF, down_shift))
        for edge, seas, first_row, shift in sides:
            order = list(range(rows)) if edge is south else list(range(rows))[::-1]
            lines = [edge[step, 0, halo, :], edge[step, 1, halo, :]]
            lines += [nat[r, strided(first_row), :] for r in order]
            for s in range(SUBSTEPS):
                moved = []
                for i in range(s, len(lines)):
                    value = staying * lines[i] + cx * pltpu.roll(lines[i], shift, 1)
                    if i > 0:
                        value = value + cy * lines[i - 1]
                    moved.append(seas[i] * value)
                lines = lines[:s] + moved
            for r, line in zip(order, lines[2:]):
                work[r, strided(first_row), :] = line

    def advance_chunk(step, h):
        for start in range(h * PER, (h + 1) * PER, CHUNKS):
            eastward = start < QUARTER
            shifts = (1, width - 1) if eastward else (width - 1, 1)

            def one(i, carry):
                advance(step, start + i, *shifts)
                return carry

            lax.fori_loop(0, CHUNKS, one, 0)

    def far_chunk(step, h):
        def one(i, carry):
            d = h * PER + i
            _, cy = courant(d)
            cube = cy * cy * cy
            halo = pl.ds(pl.multiple_of(d * NFREQ, NFREQ), NFREQ)
            work[0, strided(d), :] += (cube * far_up) * south[step, 2, halo, :]
            work[rows - 1, strided(d + HALF), :] += (cube * far_down) * north[step, 2, halo, :]
            return carry

        lax.fori_loop(0, PER, one, 0)

    def fold(value):
        return jnp.sum(value.reshape(-1, 8, width), axis=0)

    def prepare(which, low):
        for j, r in enumerate(which):
            total[r] = jnp.zeros((8, width), jnp.float32)
            for t in range(K // TILE):
                part = pl.ds(t * TILE, TILE)
                value = work[r, part, :]
                low[0, part, pl.ds(j * width, width)] = value.astype(jnp.bfloat16)
                total[r] += fold(value * value)

    def sources(which, low, finish=None):
        for sub in range(SRC_SUB):
            now, later = sub % 2, (sub + 1) % 2
            last = sub == SRC_SUB - 1
            scale = []
            for r in which:
                energy = jnp.sum(total[r], axis=0, keepdims=True) * (1.0 / K)
                factor = sea[r] / (1.0 + DAMPING * energy)
                scale.append(factor * thaw[r] if last else factor)
                total[r] = jnp.zeros((8, width), jnp.float32)
            for t in range(K // TILE):
                part = pl.ds(t * TILE, TILE)
                growth = jnp.dot(mat[part, :], low[now], preferred_element_type=jnp.float32)
                for j, r in enumerate(which):
                    value = (work[r, part, :] + gain[r] * growth[:, j * width:(j + 1) * width]) * scale[j]
                    if last:
                        nat[r, part, :] = value
                    else:
                        work[r, part, :] = value
                        low[later, part, pl.ds(j * width, width)] = value.astype(jnp.bfloat16)
                        total[r] += fold(value * value)
                if last and finish is not None:
                    finish(t)

    def out_copy(r, t):
        part = pl.ds(t * TILE, TILE)
        return pltpu.make_async_copy(nat.at[r, part], out.at[r, part], out_sem.at[r, t])

    for step in range(STEPS):
        last = step == STEPS - 1
        relay(step, 0)
        relay(step, 1)
        for h in range(CHUNKS):
            receive(step, 0, h)
            receive(step, 1, h)
            advance_chunk(step, h)
        relay(step, 2)
        if step == 0:
            mat_load.wait()
        prepare((1,), low_mid)
        sources((1,), low_mid, (lambda t: out_copy(1, t).start()) if last else None)
        if not last:
            pack(step + 1, 0)
            send(step + 1, 0)
        for h in range(CHUNKS):
            receive(step, 2, h)
            far_chunk(step, h)
        prepare((0, 2), low_out)

        def finish(t):
            out_copy(0, t).start()
            out_copy(2, t).start()

        sources((0, 2), low_out, finish if last else None)
        if not last:
            for p in range(1, rows):
                pack(step + 1, p)
                send(step + 1, p)

    @pl.when(has_north)
    def _():
        mask_up().wait_send()
        for step in range(STEPS):
            for p in range(rows):
                for h in range(CHUNKS):
                    up_copy(step, p, h).wait_send()

    @pl.when(has_south)
    def _():
        mask_down().wait_send()
        for step in range(STEPS):
            for p in range(rows):
                for h in range(CHUNKS):
                    down_copy(step, p, h).wait_send()

    for step in range(STEPS):
        for p in range(rows):
            relay_done(step, p)

    for r in range(rows):
        for t in range(K // TILE):
            out_copy(r, t).wait()


def on_device(folded, spectrum, sea_mask, ice_mask, wind, source_matrix):
    size = lax.axis_size("comp")
    spectra = spectrum.transpose(1, 0, 2)
    rows, _, width = spectra.shape
    speeds, trig = (jnp.asarray(t) for t in tables(width))
    hbm = pl.BlockSpec(memory_space=pl.ANY)
    vmem = pl.BlockSpec(memory_space=pltpu.VMEM)
    dma = pltpu.SemaphoreType.DMA
    full = pltpu.VMEM((rows, K, width), jnp.float32)
    halo = pltpu.VMEM((STEPS, rows, SIDE, width), jnp.float32)
    pieces = dma((STEPS, rows, CHUNKS))
    result = pl.pallas_call(
        functools.partial(kernel, size, folded),
        out_shape=jax.ShapeDtypeStruct(spectra.shape, jnp.float32),
        in_specs=[hbm, vmem, vmem, vmem, hbm, vmem, vmem],
        out_specs=hbm,
        scratch_shapes=[
            full, full, halo, halo, halo, halo,
            pltpu.VMEM(sea_mask.shape, jnp.int32),
            pltpu.VMEM(sea_mask.shape, jnp.int32),
            pltpu.VMEM((K, K), jnp.bfloat16),
            pltpu.VMEM((2, K, width), jnp.bfloat16),
            pltpu.VMEM((2, K, 2 * width), jnp.bfloat16),
            pltpu.VMEM((rows, 8, width), jnp.float32),
            halo,
            dma((rows,)), dma, dma((2,)), dma((2,)),
            pieces, pieces, pieces, pieces, pieces, pieces,
            dma((rows, K // TILE)),
        ],
        compiler_params=pltpu.CompilerParams(
            collective_id=0, has_side_effects=True, vmem_limit_bytes=56 * 1024 * 1024),
        name="wave",
    )(spectra, sea_mask, ice_mask, wind, source_matrix, speeds, trig)
    return result.transpose(1, 0, 2)


def is_folded(mesh):
    line = np.moveaxis(mesh.devices, mesh.axis_names.index("comp"), -1)
    line = line.reshape(-1, line.shape[-1])[0]
    places = [getattr(device, "coords", None) for device in line]
    if len(line) % FOLD or len(line) < 2 * FOLD or None in places:
        return False

    def hops(a, b):
        return sum(abs(p - q) for p, q in zip(places[a], places[b]))

    starts = range(0, len(line), FOLD)
    inside = all([hops(i, i + j) for j in range(FOLD)] == [0, 0, 1, 1] for i in starts)
    across = all(hops(i - 1, i) == 2 and hops(i - FOLD, i) == 1 for i in starts[1:])
    return inside and across


def solution(mesh):
    return jax.shard_map(
        functools.partial(on_device, is_folded(mesh)),
        mesh=mesh,
        in_specs=(
            P(None, ("grp", "comp"), None),
            P(("grp", "comp"), None),
            P(("grp", "comp"), None),
            P(("grp", "comp"), None),
            P(),
        ),
        out_specs=P(None, ("grp", "comp"), None),
        check_vma=False,
    )
```

```python
import functools

import jax
import jax.numpy as jnp
import numpy as np
from jax import lax
from jax.experimental import pallas as pl
from jax.experimental.pallas import tpu as pltpu
from jax.sharding import PartitionSpec as P

NDIR = 36
NFREQ = 32
K = NDIR * NFREQ
STEPS = 2
SUBSTEPS = 3
SRC_SUB = 3
RATE = 0.5
DAMPING = 0.5

HALF = NDIR // 2
QUARTER = HALF // 2
SIDE = HALF * NFREQ
CHUNKS = 3
PER = HALF // CHUNKS
SPAN = PER * NFREQ
TILE = 288
UP_ROW = (1, 2, 0)
DOWN_ROW = (1, 0, 2)
FOLD = 4
UNITS = 3 * CHUNKS
RELAYED = 9
MESH = pl.DeviceIdType.MESH


def tables(width):
    frequency = np.arange(NFREQ, dtype=np.float64)
    speeds = 0.6 * (0.35 + 0.65 * (NFREQ - 1 - frequency) / (NFREQ - 1))
    angles = 2.0 * np.pi * (np.arange(HALF) + 0.5) / NDIR
    trig = np.concatenate([np.abs(np.cos(angles)), np.abs(np.sin(angles))])
    spread = lambda v: np.broadcast_to(v.astype(np.float32)[:, None], (v.size, width)).copy()
    return spread(speeds), spread(trig)


def strided(d):
    return pl.ds(d, NFREQ, stride=NDIR)


def kernel(size, folded, spec, sea_ref, ice_ref, wind_ref, mat_hbm, speed_ref, trig_ref, out,
           nat, work, south, north, send_up, send_down, sea_south, sea_north, mat, low_mid, low_out,
           total, parcel, load_sem, mat_sem, mask_send, mask_recv, up_send, up_recv, down_send, down_recv, leg_recv, hop_send):
    rows, width = spec.shape[0], spec.shape[2]
    me = lax.axis_index("comp")
    has_south, has_north = me > 0, me < size - 1
    pos, fold_at, folds = me % FOLD, me // FOLD, size // FOLD
    lower, upper = pos == 0, pos == FOLD - 1
    later_fold, prior_fold = fold_at < folds - 1, fold_at > 0
    share_up = (RELAYED * (folds - 1 - fold_at) + folds // 2) // folds
    share_down = (RELAYED * fold_at + folds // 2) // folds
    greeted = has_south.astype(jnp.int32) + has_north.astype(jnp.int32)

    loads = [pltpu.make_async_copy(spec.at[r], nat.at[r], load_sem.at[r]) for r in range(rows)]
    for r in UP_ROW:
        loads[r].start()

    barrier = pltpu.get_barrier_semaphore()

    @pl.when(has_south)
    def _():
        pl.semaphore_signal(barrier, inc=1, device_id={"comp": me - 1}, device_id_type=MESH)

    @pl.when(has_north)
    def _():
        pl.semaphore_signal(barrier, inc=1, device_id={"comp": me + 1}, device_id_type=MESH)

    if folded:
        hellos = ((lower, FOLD - 1), (upper, 1 - FOLD))
        hellos += tuple((jnp.logical_and(end, near), way) for end in (lower, upper)
                        for near, way in ((later_fold, FOLD), (prior_fold, -FOLD)))
        for there, way in hellos:
            @pl.when(there)
            def _():
                pl.semaphore_signal(barrier, inc=1, device_id={"comp": me + way}, device_id_type=MESH)

            greeted += there.astype(jnp.int32)

    def relayed(share, p, h):
        return ((p * CHUNKS + h) * share) % UNITS < share

    def leg(source, step, p, h, send_sem, way):
        part = pl.ds(h * SPAN, SPAN)
        return pltpu.make_async_remote_copy(
            src_ref=source.at[step, p, part], dst_ref=parcel.at[step, p, part],
            send_sem=send_sem.at[step, p, h], recv_sem=leg_recv.at[step, p, h],
            device_id={"comp": me + way}, device_id_type=MESH)

    def hop(target, step, p, h, recv_sem, way):
        part = pl.ds(h * SPAN, SPAN)
        return pltpu.make_async_remote_copy(
            src_ref=parcel.at[step, p, part], dst_ref=target.at[step, p, part],
            send_sem=hop_send.at[step, p, h], recv_sem=recv_sem.at[step, p, h],
            device_id={"comp": me + way}, device_id_type=MESH)

    def relay(step, p):
        if not folded:
            return
        for h in range(CHUNKS):
            @pl.when(lower & later_fold & relayed(share_up, p, h))
            def _():
                leg(send_up, step, p, h, up_send, 1 - FOLD).wait_recv()
                hop(south, step, p, h, up_recv, FOLD).start()

            @pl.when(upper & prior_fold & relayed(share_down, p, h))
            def _():
                leg(send_down, step, p, h, down_send, FOLD - 1).wait_recv()
                hop(north, step, p, h, down_recv, -FOLD).start()

    def relay_done(step, p):
        if not folded:
            return
        for h in range(CHUNKS):
            @pl.when(lower & later_fold & relayed(share_up, p, h))
            def _():
                hop(south, step, p, h, up_recv, FOLD).wait_send()

            @pl.when(upper & prior_fold & relayed(share_down, p, h))
            def _():
                hop(north, step, p, h, down_recv, -FOLD).wait_send()

    def up_copy(step, p, h):
        part = pl.ds(h * SPAN, SPAN)
        return pltpu.make_async_remote_copy(
            src_ref=send_up.at[step, p, part], dst_ref=south.at[step, p, part],
            send_sem=up_send.at[step, p, h], recv_sem=up_recv.at[step, p, h],
            device_id={"comp": me + 1}, device_id_type=MESH)

    def down_copy(step, p, h):
        part = pl.ds(h * SPAN, SPAN)
        return pltpu.make_async_remote_copy(
            src_ref=send_down.at[step, p, part], dst_ref=north.at[step, p, part],
            send_sem=down_send.at[step, p, h], recv_sem=down_recv.at[step, p, h],
            device_id={"comp": me - 1}, device_id_type=MESH)

    def pack(step, p):
        for d in range(HALF):
            send_up[step, p, pl.ds(d * NFREQ, NFREQ), :] = nat[UP_ROW[p], strided(d), :]
            send_down[step, p, pl.ds(d * NFREQ, NFREQ), :] = nat[DOWN_ROW[p], strided(d + HALF), :]

    def send(step, p):
        for h in range(CHUNKS):
            by_up, by_down = has_north, has_south
            if folded:
                aside = upper & has_north & relayed(share_up, p, h)
                by_up = has_north & jnp.logical_not(aside)

                @pl.when(aside)
                def _():
                    leg(send_up, step, p, h, up_send, 1 - FOLD).start()

                aside = lower & has_south & relayed(share_down, p, h)
                by_down = has_south & jnp.logical_not(aside)

                @pl.when(aside)
                def _():
                    leg(send_down, step, p, h, down_send, FOLD - 1).start()

            @pl.when(by_up)
            def _():
                up_copy(step, p, h).start()

            @pl.when(by_down)
            def _():
                down_copy(step, p, h).start()

    def receive(step, p, h):
        @pl.when(has_south)
        def _():
            up_copy(step, p, h).wait_recv()

        @pl.when(has_north)
        def _():
            down_copy(step, p, h).wait_recv()

    def mask_up():
        return pltpu.make_async_remote_copy(
            src_ref=sea_ref, dst_ref=sea_south, send_sem=mask_send.at[0], recv_sem=mask_recv.at[0],
            device_id={"comp": me + 1}, device_id_type=MESH)

    def mask_down():
        return pltpu.make_async_remote_copy(
            src_ref=sea_ref, dst_ref=sea_north, send_sem=mask_send.at[1], recv_sem=mask_recv.at[1],
            device_id={"comp": me - 1}, device_id_type=MESH)

    loads[1].wait()
    pack(0, 0)
    pl.semaphore_wait(barrier, greeted)

    @pl.when(has_north)
    def _():
        mask_up().start()

    @pl.when(has_south)
    def _():
        mask_down().start()

    send(0, 0)
    loads[2].wait()
    loads[0].wait()
    mat_load = pltpu.make_async_copy(mat_hbm, mat, mat_sem)
    mat_load.start()
    for p in range(1, rows):
        pack(0, p)
        send(0, p)

    @pl.when(jnp.logical_not(has_south))
    def _():
        sea_south[...] = jnp.zeros_like(sea_south)
        south[...] = jnp.zeros_like(south)

    @pl.when(jnp.logical_not(has_north))
    def _():
        sea_north[...] = jnp.zeros_like(sea_north)
        north[...] = jnp.zeros_like(north)

    @pl.when(has_south)
    def _():
        mask_up().wait_recv()

    @pl.when(has_north)
    def _():
        mask_down().wait_recv()

    sea = [sea_ref[pl.ds(r, 1), :].astype(jnp.float32) for r in range(rows)]
    below = [sea_south[pl.ds(rows - 2 + r, 1), :].astype(jnp.float32) for r in range(2)]
    above = [sea_north[pl.ds(1 - r, 1), :].astype(jnp.float32) for r in range(2)]
    thaw = [1.0 - 0.5 * ice_ref[pl.ds(r, 1), :].astype(jnp.float32) for r in range(rows)]
    gain = [RATE * wind_ref[pl.ds(r, 1), :] for r in range(rows)]
    far_up = sea[0] * below[0] * below[1]
    far_down = sea[rows - 1] * above[0] * above[1]

    def courant(d):
        speed = speed_ref[...]
        return speed * trig_ref[pl.ds(d, 1), :], speed * trig_ref[pl.ds(HALF + d, 1), :]

    def advance(step, d, up_shift, down_shift):
        cx, cy = courant(d)
        staying = 1.0 - cx - cy
        halo = pl.ds(pl.multiple_of(d * NFREQ, NFREQ), NFREQ)
        sides = ((south, below + sea, d, up_shift), (north, above + sea[::-1], d + HALF, down_shift))
        for edge, seas, first_row, shift in sides:
            order = list(range(rows)) if edge is south else list(range(rows))[::-1]
            lines = [edge[step, 0, halo, :], edge[step, 1, halo, :]]
            lines += [nat[r, strided(first_row), :] for r in order]
            for s in range(SUBSTEPS):
                moved = []
                for i in range(s, len(lines)):
                    value = staying * lines[i] + cx * pltpu.roll(lines[i], shift, 1)
                    if i > 0:
                        value = value + cy * lines[i - 1]
                    moved.append(seas[i] * value)
                lines = lines[:s] + moved
            for r, line in zip(order, lines[2:]):
                work[r, strided(first_row), :] = line

    def advance_chunk(step, h):
        for start in range(h * PER, (h + 1) * PER, CHUNKS):
            eastward = start < QUARTER
            shifts = (1, width - 1) if eastward else (width - 1, 1)

            def one(i, carry):
                advance(step, start + i, *shifts)
                return carry

            lax.fori_loop(0, CHUNKS, one, 0)

    def far_chunk(step, h):
        def one(i, carry):
            d = h * PER + i
            _, cy = courant(d)
            cube = cy * cy * cy
            halo = pl.ds(pl.multiple_of(d * NFREQ, NFREQ), NFREQ)
            work[0, strided(d), :] += (cube * far_up) * south[step, 2, halo, :]
            work[rows - 1, strided(d + HALF), :] += (cube * far_down) * north[step, 2, halo, :]
            return carry

        lax.fori_loop(0, PER, one, 0)

    def fold(value):
        return jnp.sum(value.reshape(-1, 8, width), axis=0)

    def prepare(which, low):
        for j, r in enumerate(which):
            total[r] = jnp.zeros((8, width), jnp.float32)
            for t in range(K // TILE):
                part = pl.ds(t * TILE, TILE)
                value = work[r, part, :]
                low[0, part, pl.ds(j * width, width)] = value.astype(jnp.bfloat16)
                total[r] += fold(value * value)

    def sources(which, low, result):
        for sub in range(SRC_SUB):
            now, later = sub % 2, (sub + 1) % 2
            last = sub == SRC_SUB - 1
            scale = []
            for r in which:
                energy = jnp.sum(total[r], axis=0, keepdims=True) * (1.0 / K)
                factor = sea[r] / (1.0 + DAMPING * energy)
                scale.append(factor * thaw[r] if last else factor)
                total[r] = jnp.zeros((8, width), jnp.float32)
            for t in range(K // TILE):
                part = pl.ds(t * TILE, TILE)
                growth = jnp.dot(mat[part, :], low[now], preferred_element_type=jnp.float32)
                for j, r in enumerate(which):
                    value = (work[r, part, :] + gain[r] * growth[:, j * width:(j + 1) * width]) * scale[j]
                    if last:
                        result[r, part, :] = value
                    else:
                        work[r, part, :] = value
                        low[later, part, pl.ds(j * width, width)] = value.astype(jnp.bfloat16)
                        total[r] += fold(value * value)

    for step in range(STEPS):
        last = step == STEPS - 1
        relay(step, 0)
        relay(step, 1)
        for h in range(CHUNKS):
            receive(step, 0, h)
            receive(step, 1, h)
            advance_chunk(step, h)
        relay(step, 2)
        if step == 0:
            mat_load.wait()
        prepare((1,), low_mid)
        result = out if last else nat
        sources((1,), low_mid, result)
        if not last:
            pack(step + 1, 0)
            send(step + 1, 0)
        for h in range(CHUNKS):
            receive(step, 2, h)
            far_chunk(step, h)
        prepare((0, 2), low_out)

        sources((0, 2), low_out, result)
        if not last:
            for p in range(1, rows):
                pack(step + 1, p)
                send(step + 1, p)

    @pl.when(has_north)
    def _():
        mask_up().wait_send()
        for step in range(STEPS):
            for p in range(rows):
                for h in range(CHUNKS):
                    up_copy(step, p, h).wait_send()

    @pl.when(has_south)
    def _():
        mask_down().wait_send()
        for step in range(STEPS):
            for p in range(rows):
                for h in range(CHUNKS):
                    down_copy(step, p, h).wait_send()

    for step in range(STEPS):
        for p in range(rows):
            relay_done(step, p)


def on_device(folded, spectrum, sea_mask, ice_mask, wind, source_matrix):
    size = lax.axis_size("comp")
    spectra = spectrum.transpose(1, 0, 2)
    rows, _, width = spectra.shape
    speeds, trig = (jnp.asarray(t) for t in tables(width))
    hbm = pl.BlockSpec(memory_space=pl.ANY)
    vmem = pl.BlockSpec(memory_space=pltpu.VMEM)
    dma = pltpu.SemaphoreType.DMA
    full = pltpu.VMEM((rows, K, width), jnp.float32)
    halo = pltpu.VMEM((STEPS, rows, SIDE, width), jnp.float32)
    pieces = dma((STEPS, rows, CHUNKS))
    state = pl.pallas_call(
        functools.partial(kernel, size, folded),
        out_shape=pltpu.VMEM(spectra.shape, jnp.float32),
        in_specs=[hbm, vmem, vmem, vmem, hbm, vmem, vmem],
        out_specs=vmem,
        scratch_shapes=[
            full, full, halo, halo, halo, halo,
            pltpu.VMEM(sea_mask.shape, jnp.int32),
            pltpu.VMEM(sea_mask.shape, jnp.int32),
            pltpu.VMEM((K, K), jnp.bfloat16),
            pltpu.VMEM((2, K, width), jnp.bfloat16),
            pltpu.VMEM((2, K, 2 * width), jnp.bfloat16),
            pltpu.VMEM((rows, 8, width), jnp.float32),
            halo,
            dma((rows,)), dma, dma((2,)), dma((2,)),
            pieces, pieces, pieces, pieces, pieces, pieces,
        ],
        compiler_params=pltpu.CompilerParams(
            collective_id=0, has_side_effects=True, vmem_limit_bytes=58 * 1024 * 1024),
        name="wave",
    )(spectra, sea_mask, ice_mask, wind, source_matrix, speeds, trig)
    return state.transpose(1, 0, 2)


def is_folded(mesh):
    line = np.moveaxis(mesh.devices, mesh.axis_names.index("comp"), -1)
    line = line.reshape(-1, line.shape[-1])[0]
    places = [getattr(device, "coords", None) for device in line]
    if len(line) % FOLD or len(line) < 2 * FOLD or None in places:
        return False

    def hops(a, b):
        return sum(abs(p - q) for p, q in zip(places[a], places[b]))

    starts = range(0, len(line), FOLD)
    inside = all([hops(i, i + j) for j in range(FOLD)] == [0, 0, 1, 1] for i in starts)
    across = all(hops(i - 1, i) == 2 and hops(i - FOLD, i) == 1 for i in starts[1:])
    return inside and across


def solution(mesh):
    return jax.shard_map(
        functools.partial(on_device, is_folded(mesh)),
        mesh=mesh,
        in_specs=(
            P(None, ("grp", "comp"), None),
            P(("grp", "comp"), None),
            P(("grp", "comp"), None),
            P(("grp", "comp"), None),
            P(),
        ),
        out_specs=P(None, ("grp", "comp"), None),
        check_vma=False,
    )
```

```python
import functools

import jax
import jax.numpy as jnp
import numpy as np
from jax import lax
from jax.experimental import pallas as pl
from jax.experimental.pallas import tpu as pltpu
from jax.sharding import PartitionSpec as P

NDIR = 36
NFREQ = 32
K = NDIR * NFREQ
STEPS = 2
SUBSTEPS = 3
SRC_SUB = 3
RATE = 0.5
DAMPING = 0.5

HALF = NDIR // 2
QUARTER = HALF // 2
SIDE = HALF * NFREQ
CHUNKS = 6
PER = HALF // CHUNKS
SPAN = PER * NFREQ
TILE = 288
BATCH = 3
UP_ROW = (1, 2, 0)
DOWN_ROW = (1, 0, 2)
FOLD = 4
UNITS = 3 * CHUNKS
RELAYED = 16
MESH = pl.DeviceIdType.MESH


def tables(width):
    frequency = np.arange(NFREQ, dtype=np.float64)
    speeds = 0.6 * (0.35 + 0.65 * (NFREQ - 1 - frequency) / (NFREQ - 1))
    angles = 2.0 * np.pi * (np.arange(HALF) + 0.5) / NDIR
    trig = np.concatenate([np.abs(np.cos(angles)), np.abs(np.sin(angles))])
    spread = lambda v: np.broadcast_to(v.astype(np.float32)[:, None], (v.size, width)).copy()
    return spread(speeds), spread(trig)


def strided(d):
    return pl.ds(d, NFREQ, stride=NDIR)


def kernel(size, folded, spec, sea_ref, ice_ref, wind_ref, mat_hbm, speed_ref, trig_ref, out,
           nat, work, south, north, send_up, send_down, sea_south, sea_north, mat, low_mid, low_out,
           total, parcel, load_sem, mat_sem, mask_send, mask_recv, up_send, up_recv, down_send, down_recv, leg_recv, hop_send):
    rows, width = spec.shape[0], spec.shape[2]
    me = lax.axis_index("comp")
    has_south, has_north = me > 0, me < size - 1
    pos, fold_at, folds = me % FOLD, me // FOLD, size // FOLD
    lower, upper = pos == 0, pos == FOLD - 1
    later_fold, prior_fold = fold_at < folds - 1, fold_at > 0
    share_up = (RELAYED * (folds - 1 - fold_at) + folds // 2) // folds
    share_down = (RELAYED * fold_at + folds // 2) // folds
    greeted = has_south.astype(jnp.int32) + has_north.astype(jnp.int32)

    loads = [pltpu.make_async_copy(spec.at[r], nat.at[r], load_sem.at[r]) for r in range(rows)]
    for r in UP_ROW:
        loads[r].start()

    barrier = pltpu.get_barrier_semaphore()

    @pl.when(has_south)
    def _():
        pl.semaphore_signal(barrier, inc=1, device_id={"comp": me - 1}, device_id_type=MESH)

    @pl.when(has_north)
    def _():
        pl.semaphore_signal(barrier, inc=1, device_id={"comp": me + 1}, device_id_type=MESH)

    if folded:
        hellos = ((lower, FOLD - 1), (upper, 1 - FOLD))
        hellos += tuple((jnp.logical_and(end, near), way) for end in (lower, upper)
                        for near, way in ((later_fold, FOLD), (prior_fold, -FOLD)))
        for there, way in hellos:
            @pl.when(there)
            def _():
                pl.semaphore_signal(barrier, inc=1, device_id={"comp": me + way}, device_id_type=MESH)

            greeted += there.astype(jnp.int32)

    def relayed(share, p, h):
        return p * CHUNKS + h >= UNITS - share

    def leg(source, step, p, h, send_sem, way):
        part = pl.ds(h * SPAN, SPAN)
        return pltpu.make_async_remote_copy(
            src_ref=source.at[step, p, part], dst_ref=parcel.at[step, p, part],
            send_sem=send_sem.at[step, p, h], recv_sem=leg_recv.at[step, p, h],
            device_id={"comp": me + way}, device_id_type=MESH)

    def hop(target, step, p, h, recv_sem, way):
        part = pl.ds(h * SPAN, SPAN)
        return pltpu.make_async_remote_copy(
            src_ref=parcel.at[step, p, part], dst_ref=target.at[step, p, part],
            send_sem=hop_send.at[step, p, h], recv_sem=recv_sem.at[step, p, h],
            device_id={"comp": me + way}, device_id_type=MESH)

    def relay(step, p):
        if not folded:
            return
        for h in range(CHUNKS):
            @pl.when(lower & later_fold & relayed(share_up, p, h))
            def _():
                leg(send_up, step, p, h, up_send, 1 - FOLD).wait_recv()
                hop(south, step, p, h, up_recv, FOLD).start()

            @pl.when(upper & prior_fold & relayed(share_down, p, h))
            def _():
                leg(send_down, step, p, h, down_send, FOLD - 1).wait_recv()
                hop(north, step, p, h, down_recv, -FOLD).start()

    def relay_done(step, p):
        if not folded:
            return
        for h in range(CHUNKS):
            @pl.when(lower & later_fold & relayed(share_up, p, h))
            def _():
                hop(south, step, p, h, up_recv, FOLD).wait_send()

            @pl.when(upper & prior_fold & relayed(share_down, p, h))
            def _():
                hop(north, step, p, h, down_recv, -FOLD).wait_send()

    def up_copy(step, p, h):
        part = pl.ds(h * SPAN, SPAN)
        return pltpu.make_async_remote_copy(
            src_ref=send_up.at[step, p, part], dst_ref=south.at[step, p, part],
            send_sem=up_send.at[step, p, h], recv_sem=up_recv.at[step, p, h],
            device_id={"comp": me + 1}, device_id_type=MESH)

    def down_copy(step, p, h):
        part = pl.ds(h * SPAN, SPAN)
        return pltpu.make_async_remote_copy(
            src_ref=send_down.at[step, p, part], dst_ref=north.at[step, p, part],
            send_sem=down_send.at[step, p, h], recv_sem=down_recv.at[step, p, h],
            device_id={"comp": me - 1}, device_id_type=MESH)

    def pack(step, p):
        for d in range(HALF):
            send_up[step, p, pl.ds(d * NFREQ, NFREQ), :] = nat[UP_ROW[p], strided(d), :]
            send_down[step, p, pl.ds(d * NFREQ, NFREQ), :] = nat[DOWN_ROW[p], strided(d + HALF), :]

    def send(step, p):
        for h in range(CHUNKS):
            by_up, by_down = has_north, has_south
            if folded:
                aside = upper & has_north & relayed(share_up, p, h)
                by_up = has_north & jnp.logical_not(aside)

                @pl.when(aside)
                def _():
                    leg(send_up, step, p, h, up_send, 1 - FOLD).start()

                aside = lower & has_south & relayed(share_down, p, h)
                by_down = has_south & jnp.logical_not(aside)

                @pl.when(aside)
                def _():
                    leg(send_down, step, p, h, down_send, FOLD - 1).start()

            @pl.when(by_up)
            def _():
                up_copy(step, p, h).start()

            @pl.when(by_down)
            def _():
                down_copy(step, p, h).start()

    def receive(step, p, h):
        @pl.when(has_south)
        def _():
            up_copy(step, p, h).wait_recv()

        @pl.when(has_north)
        def _():
            down_copy(step, p, h).wait_recv()

    def mask_up():
        return pltpu.make_async_remote_copy(
            src_ref=sea_ref, dst_ref=sea_south, send_sem=mask_send.at[0], recv_sem=mask_recv.at[0],
            device_id={"comp": me + 1}, device_id_type=MESH)

    def mask_down():
        return pltpu.make_async_remote_copy(
            src_ref=sea_ref, dst_ref=sea_north, send_sem=mask_send.at[1], recv_sem=mask_recv.at[1],
            device_id={"comp": me - 1}, device_id_type=MESH)

    loads[1].wait()
    pack(0, 0)
    pl.semaphore_wait(barrier, greeted)

    @pl.when(has_north)
    def _():
        mask_up().start()

    @pl.when(has_south)
    def _():
        mask_down().start()

    send(0, 0)
    loads[2].wait()
    loads[0].wait()
    mat_load = pltpu.make_async_copy(mat_hbm, mat, mat_sem)
    mat_load.start()
    for p in range(1, rows):
        pack(0, p)
        send(0, p)

    @pl.when(jnp.logical_not(has_south))
    def _():
        sea_south[...] = jnp.zeros_like(sea_south)
        south[...] = jnp.zeros_like(south)

    @pl.when(jnp.logical_not(has_north))
    def _():
        sea_north[...] = jnp.zeros_like(sea_north)
        north[...] = jnp.zeros_like(north)

    @pl.when(has_south)
    def _():
        mask_up().wait_recv()

    @pl.when(has_north)
    def _():
        mask_down().wait_recv()

    sea = [sea_ref[pl.ds(r, 1), :].astype(jnp.float32) for r in range(rows)]
    below = [sea_south[pl.ds(rows - 2 + r, 1), :].astype(jnp.float32) for r in range(2)]
    above = [sea_north[pl.ds(1 - r, 1), :].astype(jnp.float32) for r in range(2)]
    thaw = [1.0 - 0.5 * ice_ref[pl.ds(r, 1), :].astype(jnp.float32) for r in range(rows)]
    gain = [RATE * wind_ref[pl.ds(r, 1), :] for r in range(rows)]
    far_up = sea[0] * below[0] * below[1]
    far_down = sea[rows - 1] * above[0] * above[1]

    def courant(d):
        speed = speed_ref[...]
        return speed * trig_ref[pl.ds(d, 1), :], speed * trig_ref[pl.ds(HALF + d, 1), :]

    def advance(step, d, up_shift, down_shift):
        cx, cy = courant(d)
        staying = 1.0 - cx - cy
        halo = pl.ds(pl.multiple_of(d * NFREQ, NFREQ), NFREQ)
        sides = ((south, below + sea, d, up_shift), (north, above + sea[::-1], d + HALF, down_shift))
        for edge, seas, first_row, shift in sides:
            order = list(range(rows)) if edge is south else list(range(rows))[::-1]
            lines = [edge[step, 0, halo, :], edge[step, 1, halo, :]]
            lines += [nat[r, strided(first_row), :] for r in order]
            for s in range(SUBSTEPS):
                moved = []
                for i in range(s, len(lines)):
                    value = staying * lines[i] + cx * pltpu.roll(lines[i], shift, 1)
                    if i > 0:
                        value = value + cy * lines[i - 1]
                    moved.append(seas[i] * value)
                lines = lines[:s] + moved
            for r, line in zip(order, lines[2:]):
                work[r, strided(first_row), :] = line

    def advance_chunk(step, h):
        for start in range(h * PER, (h + 1) * PER, BATCH):
            eastward = start < QUARTER
            shifts = (1, width - 1) if eastward else (width - 1, 1)

            def one(i, carry):
                advance(step, start + i, *shifts)
                return carry

            lax.fori_loop(0, BATCH, one, 0)

    def far_chunk(step, h):
        def one(i, carry):
            d = h * PER + i
            _, cy = courant(d)
            cube = cy * cy * cy
            halo = pl.ds(pl.multiple_of(d * NFREQ, NFREQ), NFREQ)
            work[0, strided(d), :] += (cube * far_up) * south[step, 2, halo, :]
            work[rows - 1, strided(d + HALF), :] += (cube * far_down) * north[step, 2, halo, :]
            return carry

        lax.fori_loop(0, PER, one, 0)

    def fold(value):
        return jnp.sum(value.reshape(-1, 8, width), axis=0)

    def prepare(which, low):
        for j, r in enumerate(which):
            total[r] = jnp.zeros((8, width), jnp.float32)
            for t in range(K // TILE):
                part = pl.ds(t * TILE, TILE)
                value = work[r, part, :]
                low[0, part, pl.ds(j * width, width)] = value.astype(jnp.bfloat16)
                total[r] += fold(value * value)

    def sources(which, low, result):
        for sub in range(SRC_SUB):
            now, later = sub % 2, (sub + 1) % 2
            last = sub == SRC_SUB - 1
            scale = []
            for r in which:
                energy = jnp.sum(total[r], axis=0, keepdims=True) * (1.0 / K)
                factor = sea[r] / (1.0 + DAMPING * energy)
                scale.append(factor * thaw[r] if last else factor)
                total[r] = jnp.zeros((8, width), jnp.float32)
            for t in range(K // TILE):
                part = pl.ds(t * TILE, TILE)
                growth = jnp.dot(mat[part, :], low[now], preferred_element_type=jnp.float32)
                for j, r in enumerate(which):
                    value = (work[r, part, :] + gain[r] * growth[:, j * width:(j + 1) * width]) * scale[j]
                    if last:
                        result[r, part, :] = value
                    else:
                        work[r, part, :] = value
                        low[later, part, pl.ds(j * width, width)] = value.astype(jnp.bfloat16)
                        total[r] += fold(value * value)

    for step in range(STEPS):
        last = step == STEPS - 1
        relay(step, 0)
        relay(step, 1)
        for h in range(CHUNKS):
            receive(step, 0, h)
            receive(step, 1, h)
            advance_chunk(step, h)
        relay(step, 2)
        if step == 0:
            mat_load.wait()
        prepare((1,), low_mid)
        result = out if last else nat
        sources((1,), low_mid, result)
        if not last:
            pack(step + 1, 0)
            send(step + 1, 0)
        for h in range(CHUNKS):
            receive(step, 2, h)
            far_chunk(step, h)
        prepare((0, 2), low_out)

        sources((0, 2), low_out, result)
        if not last:
            for p in range(1, rows):
                pack(step + 1, p)
                send(step + 1, p)

    @pl.when(has_north)
    def _():
        mask_up().wait_send()
        for step in range(STEPS):
            for p in range(rows):
                for h in range(CHUNKS):
                    up_copy(step, p, h).wait_send()

    @pl.when(has_south)
    def _():
        mask_down().wait_send()
        for step in range(STEPS):
            for p in range(rows):
                for h in range(CHUNKS):
                    down_copy(step, p, h).wait_send()

    for step in range(STEPS):
        for p in range(rows):
            relay_done(step, p)


def on_device(folded, spectrum, sea_mask, ice_mask, wind, source_matrix):
    size = lax.axis_size("comp")
    spectra = spectrum.transpose(1, 0, 2)
    rows, _, width = spectra.shape
    speeds, trig = (jnp.asarray(t) for t in tables(width))
    hbm = pl.BlockSpec(memory_space=pl.ANY)
    vmem = pl.BlockSpec(memory_space=pltpu.VMEM)
    dma = pltpu.SemaphoreType.DMA
    full = pltpu.VMEM((rows, K, width), jnp.float32)
    halo = pltpu.VMEM((STEPS, rows, SIDE, width), jnp.float32)
    pieces = dma((STEPS, rows, CHUNKS))
    state = pl.pallas_call(
        functools.partial(kernel, size, folded),
        out_shape=pltpu.VMEM(spectra.shape, jnp.float32),
        in_specs=[hbm, vmem, vmem, vmem, hbm, vmem, vmem],
        out_specs=vmem,
        scratch_shapes=[
            full, full, halo, halo, halo, halo,
            pltpu.VMEM(sea_mask.shape, jnp.int32),
            pltpu.VMEM(sea_mask.shape, jnp.int32),
            pltpu.VMEM((K, K), jnp.bfloat16),
            pltpu.VMEM((2, K, width), jnp.bfloat16),
            pltpu.VMEM((2, K, 2 * width), jnp.bfloat16),
            pltpu.VMEM((rows, 8, width), jnp.float32),
            halo,
            dma((rows,)), dma, dma((2,)), dma((2,)),
            pieces, pieces, pieces, pieces, pieces, pieces,
        ],
        compiler_params=pltpu.CompilerParams(
            collective_id=0, has_side_effects=True, vmem_limit_bytes=58 * 1024 * 1024),
        name="wave",
    )(spectra, sea_mask, ice_mask, wind, source_matrix, speeds, trig)
    return state.transpose(1, 0, 2)


def is_folded(mesh):
    line = np.moveaxis(mesh.devices, mesh.axis_names.index("comp"), -1)
    line = line.reshape(-1, line.shape[-1])[0]
    places = [getattr(device, "coords", None) for device in line]
    if len(line) % FOLD or len(line) < 2 * FOLD or None in places:
        return False

    def hops(a, b):
        return sum(abs(p - q) for p, q in zip(places[a], places[b]))

    starts = range(0, len(line), FOLD)
    inside = all([hops(i, i + j) for j in range(FOLD)] == [0, 0, 1, 1] for i in starts)
    across = all(hops(i - 1, i) == 2 and hops(i - FOLD, i) == 1 for i in starts[1:])
    return inside and across


def solution(mesh):
    return jax.shard_map(
        functools.partial(on_device, is_folded(mesh)),
        mesh=mesh,
        in_specs=(
            P(None, ("grp", "comp"), None),
            P(("grp", "comp"), None),
            P(("grp", "comp"), None),
            P(("grp", "comp"), None),
            P(),
        ),
        out_specs=P(None, ("grp", "comp"), None),
        check_vma=False,
    )
```
